512 devices in a mesh: chan: 32 (over y, x), row: 16 (over z, core).
Axes of the slice: x: 4, y: 8, z: 8, core: 2. Of those that a mesh axis runs over, the one named last changes fastest.
Arguments:
- amplitudes: bfloat16 [32, 3072, 2048], P('chan', 'row'), may hold values from -6 to 6
- interaction: bfloat16 [32, 2048, 2048], P('chan', 'row'), as said below
- weights6j: float32 [32, 2048], P('chan'), may hold values from -1.5 to 1.5
- column_order: int32 [32, 2048], P('chan'), may hold values from 0 to 2047, each once within a row
- row_counts: int32 [32], P('chan'), may hold values from 768 to 3072, as said below
Outputs:
- pp_update: bfloat16 [32, 3072, 2048], P('chan', 'row')
The draws below stay inside these ranges and needn't reach their ends.
Inputs may be any that keep to these rules, and one draw needn't show every extreme that they name: Each channel's interaction block is symmetric. `row_counts`: some channel has all 3072 rows live and some channel exactly 768 in every draw.
All inputs are finite; a program needn't handle non-finite values.
Results may differ from the reference program's by a relative error of at most 0.005.
Values may be sent and summed in bfloat16 or wider, within the bound.
No kernel may reach another device: no remote copies, remote signals or barrier semaphores. Data moves between devices by JAX's collectives and lax.ppermute only.
A program may use at most 64 MiB of HBM per device.

```python
import math
import jax
import jax.numpy as jnp
from jax import lax

ORDER = 2048
CHANNELS = 32
ROWS = 3072
GROUP = 64


def draw_interaction(key, part):
    shape = (CHANNELS, ORDER, ORDER)
    entries = jax.random.normal(key, shape, jnp.float32)
    summed = (entries + jnp.swapaxes(entries, 1, 2)) * 0.5 ** 0.5
    return (summed / math.sqrt(ORDER)).astype(jnp.bfloat16)


def draw_row_counts(key, part):
    counts = jax.random.randint(key, (CHANNELS,), ROWS // 4, ROWS + 1)
    order = jax.random.permutation(jax.random.fold_in(key, 7), CHANNELS)
    counts = counts.at[order[0]].set(ROWS)
    counts = counts.at[order[1]].set(ROWS // 4)
    return counts.astype(jnp.int32)


def level_of(key, extent, pieces, low, largest):
    level, own = 1.0, jax.random.fold_in(key, 6)
    for axis_at, blocks in pieces:
        heights = jnp.exp(jax.random.uniform(jax.random.fold_in(own, axis_at), (blocks,), jnp.float32, low / len(pieces), largest / len(pieces)))
        level = level * jnp.repeat(heights, extent[axis_at] // blocks).reshape([-1 if axis == axis_at else 1 for axis in range(len(extent))])
    return level


def gaussian(own_key, extent, scale, most, cuts=(), kind=jnp.bfloat16):
    values = jax.random.normal(own_key, extent, jnp.float32) * scale
    if len(cuts) > 0:
        values = level_of(own_key, extent, cuts, -0.22, 0.18) * values
    return jnp.clip(values, min=-most, max=most).astype(kind)


def setup_inputs(seed: int = 0) -> dict:
    arg_keys = jax.random.split(jax.random.key(seed), 6)
    amplitudes = gaussian(arg_keys[0], (CHANNELS, ROWS, ORDER), 1.0, 6.0, ((0, 32), (1, 16)))
    interaction = draw_interaction(jax.random.fold_in(arg_keys[5], 71), 0)
    weights6j = jnp.clip(jax.random.uniform(arg_keys[2], (CHANNELS, ORDER), jnp.float32, -1.5, 1.5) * level_of(arg_keys[2], (CHANNELS, ORDER), ((0, 32),), -0.4, 0.0), -1.5, 1.5)
    column_order = jax.vmap(lambda own: jax.random.permutation(own, ORDER))(jax.random.split(arg_keys[3], CHANNELS)).reshape((CHANNELS, ORDER)).astype(jnp.int32)
    row_counts = draw_row_counts(jax.random.fold_in(arg_keys[5], 71), 0)
    return {"amplitudes": amplitudes, "interaction": interaction, "weights6j": weights6j, "column_order": column_order, "row_counts": row_counts}


def regroup(blocks):
    return blocks.reshape(CHANNELS, ROWS, CHANNELS, GROUP).transpose(2, 1, 0, 3).reshape(CHANNELS, ROWS, ORDER)


def per_channel(packed):
    ph_block, v_matrix, w_column, col_order, row_limit = packed
    live_rows = jnp.arange(ROWS, dtype=jnp.int32) < row_limit
    taken = jnp.take(ph_block, col_order, axis=1).astype(jnp.float32) * w_column[None, :]
    recoupled = jnp.where(live_rows[:, None], taken, jnp.float32(0.0)).astype(jnp.bfloat16)
    product = jnp.dot(recoupled.astype(jnp.float32), v_matrix.astype(jnp.float32), precision=lax.Precision.HIGHEST)
    scaled = (product * w_column[None, :]).astype(jnp.bfloat16)
    inverse = jnp.zeros((ORDER,), jnp.int32).at[col_order].set(jnp.arange(ORDER, dtype=jnp.int32))
    return jnp.take(scaled, inverse, axis=1)


def reference(amplitudes, interaction, weights6j, column_order, row_counts):
    gathered = regroup(amplitudes)
    restored = lax.map(per_channel, (gathered, interaction, weights6j, column_order, row_counts))
    return regroup(restored)
```

```python
import jax
import jax.numpy as jnp
from jax import lax
from jax.experimental import pallas as pl
from jax.experimental.pallas import tpu as pltpu
from jax.sharding import PartitionSpec as P

VMEM_LIMIT = 56 * 1024 * 1024
TILE = 256


def call(body, out_shape, in_specs, scratch=()):
    return pl.pallas_call(
        body,
        out_shape=out_shape,
        in_specs=in_specs,
        out_specs=pl.BlockSpec(memory_space=pltpu.VMEM),
        scratch_shapes=list(scratch),
        compiler_params=pltpu.CompilerParams(vmem_limit_bytes=VMEM_LIMIT),
    )


def vmem():
    return pl.BlockSpec(memory_space=pltpu.VMEM)


def smem():
    return pl.BlockSpec(memory_space=pltpu.SMEM)


def anywhere():
    return pl.BlockSpec(memory_space=pl.ANY)


def swap_halves(upper, lower):
    low_lane = lax.broadcasted_iota(jnp.int32, upper.shape, 1) < 64
    first = jnp.where(low_lane, upper, pltpu.roll(lower, 64, 1))
    second = jnp.where(low_lane, pltpu.roll(upper, 64, 1), lower)
    return first, second


def pack_body(block_ref, out_ref):
    half = block_ref.shape[0] // 2
    for pair in range(out_ref.shape[0] // 2):
        lanes = pl.ds(pair * 128, 128)
        first, second = swap_halves(
            block_ref[:half, lanes].astype(jnp.float32), block_ref[half:, lanes].astype(jnp.float32)
        )
        out_ref[2 * pair] = first.astype(out_ref.dtype)
        out_ref[2 * pair + 1] = second.astype(out_ref.dtype)


def unpack_body(groups_ref, out_ref):
    half = groups_ref.shape[1]
    for pair in range(groups_ref.shape[0] // 2):
        lanes = pl.ds(pair * 128, 128)
        upper, lower = swap_halves(
            groups_ref[2 * pair].astype(jnp.float32), groups_ref[2 * pair + 1].astype(jnp.float32)
        )
        out_ref[:half, lanes] = upper.astype(out_ref.dtype)
        out_ref[half:, lanes] = lower.astype(out_ref.dtype)


def selection(order, first):
    rows = lax.broadcasted_iota(jnp.int32, (TILE, order.shape[1]), 0) + first
    return jnp.where(rows == order, 1.0, 0.0).astype(jnp.bfloat16)


def recouple_body(live_ref, groups_ref, order_ref, weight_ref, out_ref, gathered):
    unpack_body(groups_ref, gathered)
    row_count, col_count = out_ref.shape
    live = lax.broadcasted_iota(jnp.int32, (row_count, TILE), 0) < live_ref[0]
    for at in range(0, col_count, TILE):
        order = order_ref[:, at : at + TILE]
        rows = lax.broadcasted_iota(jnp.int32, (col_count, TILE), 0)
        picks = jnp.where(rows == order, 1.0, 0.0).astype(jnp.bfloat16)
        taken = jnp.dot(gathered[...], picks, preferred_element_type=jnp.float32)
        taken = taken * weight_ref[:, at : at + TILE]
        out_ref[:, at : at + TILE] = jnp.where(live, taken, 0.0).astype(out_ref.dtype)


def product_body(
    recoupled_ref, panel_ref, order_ref, weight_ref, out_ref, panel, scaled, restored, sems
):
    col_count = recoupled_ref.shape[1]
    steps = col_count // TILE
    copies = [
        pltpu.make_async_copy(
            panel_ref.at[:, pl.ds(step * TILE, TILE)], panel.at[step], sems.at[step]
        )
        for step in range(steps)
    ]
    for copy in copies:
        copy.start()
    for step in range(steps):
        at = step * TILE
        copies[step].wait()
        product = jnp.dot(recoupled_ref[...], panel[step], preferred_element_type=jnp.float32)
        scaled[:, at : at + TILE] = (product * weight_ref[:, at : at + TILE]).astype(scaled.dtype)
    for step in range(steps):
        at = step * TILE
        picks = selection(order_ref[...], at)
        placed = lax.dot_general(
            scaled[...], picks, (((1,), (1,)), ((), ())), preferred_element_type=jnp.float32
        )
        restored[:, at : at + TILE] = placed.astype(restored.dtype)
    pack_body(restored, out_ref)


def per_device(amplitudes, interaction, weights6j, column_order, row_counts):
    own_block = amplitudes[0]
    row_count, col_count = own_block.shape
    chan_count = lax.axis_size("chan")
    dtype = own_block.dtype
    packed_shape = (chan_count, row_count // 2, 128)
    packed = jax.ShapeDtypeStruct(packed_shape, dtype)
    flat = jax.ShapeDtypeStruct((row_count, col_count), dtype)
    steps = col_count // TILE

    v_panel = lax.all_gather(interaction[0], "row", axis=0, tiled=True)
    sent = call(pack_body, packed, [vmem()])(own_block)
    groups = lax.all_to_all(sent, "chan", split_axis=0, concat_axis=0, tiled=True)
    live_rows = row_counts - lax.axis_index("row") * row_count
    recoupled = call(
        recouple_body, flat, [smem(), vmem(), vmem(), vmem()], [pltpu.VMEM(flat.shape, dtype)]
    )(live_rows, groups, column_order, weights6j)
    restored = call(
        product_body,
        packed,
        [vmem(), anywhere(), vmem(), vmem()],
        [
            pltpu.VMEM((steps, col_count, TILE), dtype),
            pltpu.VMEM(flat.shape, dtype),
            pltpu.VMEM(flat.shape, dtype),
            pltpu.SemaphoreType.DMA((steps,)),
        ],
    )(recoupled, v_panel, column_order, weights6j)
    returned = lax.all_to_all(restored, "chan", split_axis=0, concat_axis=0, tiled=True)
    return call(unpack_body, flat, [vmem()])(returned)[None]


def solution(mesh):
    in_specs = (
        P("chan", "row", None),
        P("chan", "row", None),
        P("chan", None),
        P("chan", None),
        P("chan"),
    )
    out_specs = P("chan", "row", None)
    return jax.shard_map(
        per_device, mesh=mesh, in_specs=in_specs, out_specs=out_specs, check_vma=False
    )
```

```python
import jax
import jax.numpy as jnp
from jax import lax
from jax.experimental import pallas as pl
from jax.experimental.pallas import tpu as pltpu
from jax.sharding import PartitionSpec as P

VMEM_LIMIT = 56 * 1024 * 1024
TILE = 256
BLOCK = 128


def call(body, out_shape, in_specs, scratch=()):
    return pl.pallas_call(
        body,
        out_shape=out_shape,
        in_specs=in_specs,
        out_specs=pl.BlockSpec(memory_space=pltpu.VMEM),
        scratch_shapes=list(scratch),
        compiler_params=pltpu.CompilerParams(vmem_limit_bytes=VMEM_LIMIT),
    )


def vmem():
    return pl.BlockSpec(memory_space=pltpu.VMEM)


def smem():
    return pl.BlockSpec(memory_space=pltpu.SMEM)


def anywhere():
    return pl.BlockSpec(memory_space=pl.ANY)


def swap_halves(upper, lower):
    low_lane = lax.broadcasted_iota(jnp.int32, upper.shape, 1) < 64
    first = jnp.where(low_lane, upper, pltpu.roll(lower, 64, 1))
    second = jnp.where(low_lane, pltpu.roll(upper, 64, 1), lower)
    return first, second


def pack_body(block_ref, out_ref):
    half = block_ref.shape[0] // 2
    for pair in range(out_ref.shape[0] // 2):
        lanes = pl.ds(pair * 128, 128)
        first, second = swap_halves(
            block_ref[:half, lanes].astype(jnp.float32), block_ref[half:, lanes].astype(jnp.float32)
        )
        out_ref[2 * pair] = first.astype(out_ref.dtype)
        out_ref[2 * pair + 1] = second.astype(out_ref.dtype)


def unpack_body(groups_ref, out_ref):
    half = groups_ref.shape[1]
    for pair in range(groups_ref.shape[0] // 2):
        lanes = pl.ds(pair * 128, 128)
        upper, lower = swap_halves(
            groups_ref[2 * pair].astype(jnp.float32), groups_ref[2 * pair + 1].astype(jnp.float32)
        )
        out_ref[:half, lanes] = upper.astype(out_ref.dtype)
        out_ref[half:, lanes] = lower.astype(out_ref.dtype)


def selection(order, first):
    rows = lax.broadcasted_iota(jnp.int32, (TILE, order.shape[1]), 0) + first
    return jnp.where(rows == order, 1.0, 0.0).astype(jnp.bfloat16)


def recouple_body(live_ref, groups_ref, order_ref, weight_ref, out_ref, gathered):
    unpack_body(groups_ref, gathered)
    row_count, col_count = out_ref.shape
    live = lax.broadcasted_iota(jnp.int32, (row_count, TILE), 0) < live_ref[0]
    for at in range(0, col_count, TILE):
        order = order_ref[:, at : at + TILE]
        rows = lax.broadcasted_iota(jnp.int32, (col_count, TILE), 0)
        picks = jnp.where(rows == order, 1.0, 0.0).astype(jnp.bfloat16)
        taken = jnp.dot(gathered[...], picks, preferred_element_type=jnp.float32)
        taken = taken * weight_ref[:, at : at + TILE]
        out_ref[:, at : at + TILE] = jnp.where(live, taken, 0.0).astype(out_ref.dtype)


def halve_body(start_ref, panel_ref, out_ref):
    blocks = panel_ref.shape[1] // BLOCK
    for step in range(out_ref.shape[1] // BLOCK):
        at = pl.multiple_of((start_ref[0] + step) % blocks * BLOCK, BLOCK)
        out_ref[:, step * BLOCK : (step + 1) * BLOCK] = panel_ref[:, pl.ds(at, BLOCK)]


def product_body(
    recoupled_ref, halves_ref, order_ref, weight_ref, out_ref, panel, scaled, restored, sems
):
    col_count = recoupled_ref.shape[1]
    blocks, width = col_count // BLOCK, halves_ref.shape[1]
    copies = []
    for block in range(blocks):
        rows = pl.ds(block * BLOCK, BLOCK)
        inside = min(width, col_count - block * BLOCK)
        parts = [(0, block * BLOCK, inside)]
        if inside < width:
            parts.append((inside, 0, width - inside))
        copies.append(
            [
                pltpu.make_async_copy(
                    halves_ref.at[rows, pl.ds(source, size)],
                    panel.at[rows, pl.ds(target, size)],
                    sems.at[2 * block + part],
                )
                for part, (source, target, size) in enumerate(parts)
            ]
        )
        for copy in copies[-1]:
            copy.start()
    for block in range(blocks):
        for copy in copies[block]:
            copy.wait()
        own = slice(block * BLOCK, (block + 1) * BLOCK)
        for step in range(1, blocks - width // BLOCK + 1):
            other = (block + step) % blocks
            there = slice(other * BLOCK, (other + 1) * BLOCK)
            panel[there, own] = panel[own, there].T
    for at in range(0, col_count, TILE):
        product = jnp.dot(
            recoupled_ref[...], panel[:, at : at + TILE], preferred_element_type=jnp.float32
        )
        scaled[:, at : at + TILE] = (product * weight_ref[:, at : at + TILE]).astype(scaled.dtype)
    for at in range(0, col_count, TILE):
        picks = selection(order_ref[...], at)
        placed = lax.dot_general(
            scaled[...], picks, (((1,), (1,)), ((), ())), preferred_element_type=jnp.float32
        )
        restored[:, at : at + TILE] = placed.astype(restored.dtype)
    pack_body(restored, out_ref)


def per_device(amplitudes, interaction, weights6j, column_order, row_counts):
    own_block = amplitudes[0]
    row_count, col_count = own_block.shape
    chan_count = lax.axis_size("chan")
    dtype = own_block.dtype
    packed_shape = (chan_count, row_count // 2, 128)
    packed = jax.ShapeDtypeStruct(packed_shape, dtype)
    flat = jax.ShapeDtypeStruct((row_count, col_count), dtype)
    blocks = col_count // BLOCK

    row_at = lax.axis_index("row")
    half = jax.ShapeDtypeStruct((BLOCK, (blocks // 2 + 1) * BLOCK), dtype)
    own_half = call(halve_body, half, [smem(), vmem()])(row_at[None], interaction[0])
    halves = lax.all_gather(own_half, "row", axis=0, tiled=True)
    sent = call(pack_body, packed, [vmem()])(own_block)
    groups = lax.all_to_all(sent, "chan", split_axis=0, concat_axis=0, tiled=True)
    live_rows = row_counts - row_at * row_count
    recoupled = call(
        recouple_body, flat, [smem(), vmem(), vmem(), vmem()], [pltpu.VMEM(flat.shape, dtype)]
    )(live_rows, groups, column_order, weights6j)
    restored = call(
        product_body,
        packed,
        [vmem(), anywhere(), vmem(), vmem()],
        [
            pltpu.VMEM((col_count, col_count), dtype),
            pltpu.VMEM(flat.shape, dtype),
            pltpu.VMEM(flat.shape, dtype),
            pltpu.SemaphoreType.DMA((2 * blocks,)),
        ],
    )(recoupled, halves, column_order, weights6j)
    returned = lax.all_to_all(restored, "chan", split_axis=0, concat_axis=0, tiled=True)
    return call(unpack_body, flat, [vmem()])(returned)[None]


def solution(mesh):
    in_specs = (
        P("chan", "row", None),
        P("chan", "row", None),
        P("chan", None),
        P("chan", None),
        P("chan"),
    )
    out_specs = P("chan", "row", None)
    return jax.shard_map(
        per_device, mesh=mesh, in_specs=in_specs, out_specs=out_specs, check_vma=False
    )
```

```python
import jax
import jax.numpy as jnp
from jax import lax
from jax.experimental import pallas as pl
from jax.experimental.pallas import tpu as pltpu
from jax.sharding import PartitionSpec as P

VMEM_LIMIT = 28 * 1024 * 1024
TILE = 256
BLOCK = 128


def call(body, out_shape, in_specs, scratch=()):
    return pl.pallas_call(
        body,
        out_shape=out_shape,
        in_specs=in_specs,
        out_specs=jax.tree.map(lambda _: vmem(), out_shape),
        scratch_shapes=list(scratch),
        compiler_params=pltpu.CompilerParams(vmem_limit_bytes=VMEM_LIMIT),
    )


def near_core(array):
    return pltpu.with_memory_space_constraint(array, pltpu.VMEM)


def vmem():
    return pl.BlockSpec(memory_space=pltpu.VMEM)


def smem():
    return pl.BlockSpec(memory_space=pltpu.SMEM)


def anywhere():
    return pl.BlockSpec(memory_space=pl.ANY)


def swap_halves(upper, lower):
    low_lane = lax.broadcasted_iota(jnp.int32, upper.shape, 1) < 64
    first = jnp.where(low_lane, upper, pltpu.roll(lower, 64, 1))
    second = jnp.where(low_lane, pltpu.roll(upper, 64, 1), lower)
    return first, second


def pack_body(block_ref, out_ref):
    half = block_ref.shape[0] // 2
    for pair in range(out_ref.shape[0] // 2):
        lanes = pl.ds(pair * 128, 128)
        first, second = swap_halves(
            block_ref[:half, lanes].astype(jnp.float32), block_ref[half:, lanes].astype(jnp.float32)
        )
        out_ref[2 * pair] = first.astype(out_ref.dtype)
        out_ref[2 * pair + 1] = second.astype(out_ref.dtype)


def unpack_body(groups_ref, out_ref):
    half = groups_ref.shape[1]
    for pair in range(groups_ref.shape[0] // 2):
        lanes = pl.ds(pair * 128, 128)
        upper, lower = swap_halves(
            groups_ref[2 * pair].astype(jnp.float32), groups_ref[2 * pair + 1].astype(jnp.float32)
        )
        out_ref[:half, lanes] = upper.astype(out_ref.dtype)
        out_ref[half:, lanes] = lower.astype(out_ref.dtype)


def selection(order, first):
    rows = lax.broadcasted_iota(jnp.int32, (TILE, order.shape[1]), 0) + first
    return jnp.where(rows == order, 1.0, 0.0).astype(jnp.bfloat16)


def recouple_body(live_ref, groups_ref, order_ref, weight_ref, out_ref, gathered):
    unpack_body(groups_ref, gathered)
    row_count, col_count = out_ref.shape
    live = lax.broadcasted_iota(jnp.int32, (row_count, TILE), 0) < live_ref[0]
    for at in range(0, col_count, TILE):
        order = order_ref[:, at : at + TILE]
        rows = lax.broadcasted_iota(jnp.int32, (col_count, TILE), 0)
        picks = jnp.where(rows == order, 1.0, 0.0).astype(jnp.bfloat16)
        taken = jnp.dot(gathered[...], picks, preferred_element_type=jnp.float32)
        taken = taken * weight_ref[:, at : at + TILE]
        out_ref[:, at : at + TILE] = jnp.where(live, taken, 0.0).astype(out_ref.dtype)


def rotated(table_ref, first, out_ref):
    blocks = out_ref.shape[1] // BLOCK
    for step in range(blocks):
        at = pl.multiple_of((first + step) % blocks * BLOCK, BLOCK)
        out_ref[:, step * BLOCK : (step + 1) * BLOCK] = table_ref[:, pl.ds(at, BLOCK)]


def halve_body(row_ref, panel_ref, out_ref):
    blocks = panel_ref.shape[1] // BLOCK
    for step in range(out_ref.shape[1] // BLOCK):
        at = pl.multiple_of((row_ref[0] + step) % blocks * BLOCK, BLOCK)
        out_ref[:, step * BLOCK : (step + 1) * BLOCK] = panel_ref[:, pl.ds(at, BLOCK)]


def send_body(row_ref, block_ref, order_ref, weight_ref, out_ref, order_out, weight_out):
    pack_body(block_ref, out_ref)
    first = row_ref[0] - row_ref[0] % 2
    rotated(order_ref, first, order_out)
    rotated(weight_ref, first, weight_out)


def stack_body(*refs):
    pieces, out_ref = refs[:-1], refs[-1]
    for number, piece in enumerate(pieces):
        out_ref[number * BLOCK : (number + 1) * BLOCK] = piece[...]


def product_body(core_ref, recoupled_ref, order_ref, weight_ref, own_ref, partner_ref, *refs):
    row_count, col_count = recoupled_ref.shape
    blocks = col_count // BLOCK
    out_ref, panel, scaled, restored = refs
    width = own_ref.shape[1]

    def place(stack, parity):
        for number, chip in enumerate(CHIPS):
            first = (2 * (chip % (blocks // 2)) + parity) * BLOCK
            inside = min(width, col_count - first)
            source = slice(number * BLOCK, (number + 1) * BLOCK)
            panel[first : first + BLOCK, first : first + inside] = stack[source, :inside]
            if inside < width:
                panel[first : first + BLOCK, : width - inside] = stack[source, inside:]

    for parity in range(2):

        @pl.when(core_ref[0] == parity)
        def _(parity=parity):
            place(own_ref, parity)
            place(partner_ref, 1 - parity)

    for block in range(blocks):
        own = slice(block * BLOCK, (block + 1) * BLOCK)
        for step in range(1, blocks - width // BLOCK + 1):
            other = (block + step) % blocks
            there = slice(other * BLOCK, (other + 1) * BLOCK)
            panel[there, own] = panel[own, there].T
    for at in range(0, col_count, TILE):
        product = jnp.dot(
            recoupled_ref[...], panel[:, at : at + TILE], preferred_element_type=jnp.float32
        )
        scaled[:, at : at + TILE] = (product * weight_ref[:, at : at + TILE]).astype(scaled.dtype)
    for at in range(0, col_count, TILE):
        picks = selection(order_ref[...], at)
        placed = lax.dot_general(
            scaled[...], picks, (((1,), (1,)), ((), ())), preferred_element_type=jnp.float32
        )
        restored[:, at : at + TILE] = placed.astype(restored.dtype)
    pack_body(restored, out_ref)


CHIPS = (0, -1, 1, -2, 2, -3, 3, 4)


def per_device(amplitudes, interaction, weights6j, column_order, row_counts):
    own_block = amplitudes[0]
    row_count, col_count = own_block.shape
    chan_count = lax.axis_size("chan")
    dtype = own_block.dtype
    packed_shape = (chan_count, row_count // 2, 128)
    packed = jax.ShapeDtypeStruct(packed_shape, dtype)
    flat = jax.ShapeDtypeStruct((row_count, col_count), dtype)
    blocks = col_count // BLOCK

    row_at = lax.axis_index("row")
    rows = lax.axis_size("row")
    core = row_at % 2
    half = jax.ShapeDtypeStruct((BLOCK, (blocks // 2 + 1) * BLOCK), dtype)
    own_half = call(halve_body, half, [smem(), vmem()])(row_at[None], interaction[0])

    def hop(far):
        return [(row, (row + 2 * far) % rows) for row in range(rows)]

    swap = [(row, row ^ 1) for row in range(rows)]
    sent, order, weight = call(
        send_body,
        (
            packed,
            jax.ShapeDtypeStruct(column_order.shape, column_order.dtype),
            jax.ShapeDtypeStruct(weights6j.shape, weights6j.dtype),
        ),
        [smem(), vmem(), vmem(), vmem()],
    )(row_at[None], own_block, column_order, weights6j)
    from_below = [lax.ppermute(own_half, "row", hop(far)) for far in (1, 2)]
    from_above = [lax.ppermute(own_half, "row", hop(-far)) for far in (1, 2)]
    sent = near_core(sent)
    groups = lax.all_to_all(sent, "chan", split_axis=0, concat_axis=0, tiled=True)
    third_below = lax.ppermute(from_below[1], "row", hop(1))
    third_above = lax.ppermute(from_above[1], "row", hop(-1))
    apart = list(zip(hop(2), hop(-2)))
    passed = jnp.where(core == 0, from_below[1], from_above[1])
    opposite = lax.ppermute(passed, "row", [pair[row % 2] for row, pair in enumerate(apart)])
    live_rows = row_counts - row_at * row_count
    recoupled = call(
        recouple_body, flat, [smem(), vmem(), vmem(), vmem()], [pltpu.VMEM(flat.shape, dtype)]
    )(live_rows, near_core(groups), order, weight)
    third_below, recoupled = lax.optimization_barrier((third_below, recoupled))
    pieces = [own_half, from_below[0], from_above[0], from_below[1], from_above[1]]
    pieces += [third_below, third_above, opposite]
    stack_shape = jax.ShapeDtypeStruct((len(pieces) * BLOCK, half.shape[1]), dtype)
    stack = call(stack_body, stack_shape, [vmem()] * len(pieces))(*map(near_core, pieces))
    stack = near_core(stack)
    partner = near_core(lax.ppermute(stack, "row", swap))
    restored = call(
        product_body,
        packed,
        [smem(), *[vmem()] * 5],
        [
            pltpu.VMEM((col_count, col_count), dtype),
            pltpu.VMEM(flat.shape, dtype),
            pltpu.VMEM(flat.shape, dtype),
        ],
    )(core[None], near_core(recoupled), order, weight, stack, partner)
    restored = near_core(restored)
    returned = lax.all_to_all(restored, "chan", split_axis=0, concat_axis=0, tiled=True)
    return call(unpack_body, flat, [vmem()])(near_core(returned))[None]


def solution(mesh):
    in_specs = (
        P("chan", "row", None),
        P("chan", "row", None),
        P("chan", None),
        P("chan", None),
        P("chan"),
    )
    out_specs = P("chan", "row", None)
    return jax.shard_map(
        per_device, mesh=mesh, in_specs=in_specs, out_specs=out_specs, check_vma=False
    )
```

```python
import jax
import jax.numpy as jnp
from jax import lax
from jax.experimental import pallas as pl
from jax.experimental.pallas import tpu as pltpu
from jax.sharding import PartitionSpec as P

VMEM_LIMIT = 28 * 1024 * 1024
TILE = 256
BLOCK = 128


def call(body, out_shape, in_specs, scratch=()):
    return pl.pallas_call(
        body,
        out_shape=out_shape,
        in_specs=in_specs,
        out_specs=jax.tree.map(lambda _: vmem(), out_shape),
        scratch_shapes=list(scratch),
        compiler_params=pltpu.CompilerParams(vmem_limit_bytes=VMEM_LIMIT),
    )


def near_core(array):
    return pltpu.with_memory_space_constraint(array, pltpu.VMEM)


def vmem():
    return pl.BlockSpec(memory_space=pltpu.VMEM)


def smem():
    return pl.BlockSpec(memory_space=pltpu.SMEM)


def anywhere():
    return pl.BlockSpec(memory_space=pl.ANY)


def swap_halves(upper, lower):
    low_lane = lax.broadcasted_iota(jnp.int32, upper.shape, 1) < 64
    first = jnp.where(low_lane, upper, pltpu.roll(lower, 64, 1))
    second = jnp.where(low_lane, pltpu.roll(upper, 64, 1), lower)
    return first, second


def pack_body(block_ref, out_ref):
    half = block_ref.shape[0] // 2
    for pair in range(out_ref.shape[0] // 2):
        lanes = pl.ds(pair * 128, 128)
        first, second = swap_halves(
            block_ref[:half, lanes].astype(jnp.float32), block_ref[half:, lanes].astype(jnp.float32)
        )
        out_ref[2 * pair] = first.astype(out_ref.dtype)
        out_ref[2 * pair + 1] = second.astype(out_ref.dtype)


def unpack_body(groups_ref, out_ref):
    half = groups_ref.shape[1]
    for pair in range(groups_ref.shape[0] // 2):
        lanes = pl.ds(pair * 128, 128)
        upper, lower = swap_halves(
            groups_ref[2 * pair].astype(jnp.float32), groups_ref[2 * pair + 1].astype(jnp.float32)
        )
        out_ref[:half, lanes] = upper.astype(out_ref.dtype)
        out_ref[half:, lanes] = lower.astype(out_ref.dtype)


def selection(order, first):
    rows = lax.broadcasted_iota(jnp.int32, (TILE, order.shape[1]), 0) + first
    return jnp.where(rows == order, 1.0, 0.0).astype(jnp.bfloat16)


def rotated(table_ref, first, out_ref):
    blocks = out_ref.shape[1] // BLOCK
    for step in range(blocks):
        at = pl.multiple_of((first + step) % blocks * BLOCK, BLOCK)
        out_ref[:, step * BLOCK : (step + 1) * BLOCK] = table_ref[:, pl.ds(at, BLOCK)]


def recouple_body(
    live_ref, row_ref, groups_ref, order_in, weight_in, out_ref, order_ref, weight_ref, gathered
):
    first = row_ref[0] - row_ref[0] % 2
    rotated(order_in, first, order_ref)
    rotated(weight_in, first, weight_ref)
    unpack_body(groups_ref, gathered)
    row_count, col_count = out_ref.shape
    live = lax.broadcasted_iota(jnp.int32, (row_count, TILE), 0) < live_ref[0]
    for at in range(0, col_count, TILE):
        order = order_ref[:, at : at + TILE]
        rows = lax.broadcasted_iota(jnp.int32, (col_count, TILE), 0)
        picks = jnp.where(rows == order, 1.0, 0.0).astype(jnp.bfloat16)
        taken = jnp.dot(gathered[...], picks, preferred_element_type=jnp.float32)
        taken = taken * weight_ref[:, at : at + TILE]
        out_ref[:, at : at + TILE] = jnp.where(live, taken, 0.0).astype(out_ref.dtype)


def halve_body(row_ref, panel_ref, out_ref):
    blocks = panel_ref.shape[1] // BLOCK
    for step in range(out_ref.shape[1] // BLOCK):
        at = pl.multiple_of((row_ref[0] + step) % blocks * BLOCK, BLOCK)
        out_ref[:, step * BLOCK : (step + 1) * BLOCK] = panel_ref[:, pl.ds(at, BLOCK)]


def stack_body(*refs):
    pieces, out_ref = refs[:-1], refs[-1]
    for number, piece in enumerate(pieces):
        out_ref[number * BLOCK : (number + 1) * BLOCK] = piece[...]


def product_body(core_ref, recoupled_ref, order_ref, weight_ref, *refs):
    row_count, col_count = recoupled_ref.shape
    blocks = col_count // BLOCK
    own_near, partner_near, own_far, partner_far, out_ref, panel, scaled, restored, sems = refs
    width = own_near.shape[1]

    def bring(stack, chips, parity):
        copies = []
        for number, chip in enumerate(chips):
            first = (2 * (chip % (blocks // 2)) + parity) * BLOCK
            inside = min(width, col_count - first)
            source, target = pl.ds(number * BLOCK, BLOCK), pl.ds(first, BLOCK)
            parts = [(0, first, inside)]
            if inside < width:
                parts.append((inside, 0, width - inside))
            for left, column, size in parts:
                copies.append(
                    pltpu.make_async_copy(
                        stack.at[source, pl.ds(left, size)],
                        panel.at[target, pl.ds(column, size)],
                        sems.at[len(copies)],
                    )
                )
        for copy in copies:
            copy.start()
        return copies

    def place(stack, chips, parity):
        for number, chip in enumerate(chips):
            first = (2 * (chip % (blocks // 2)) + parity) * BLOCK
            inside = min(width, col_count - first)
            source = slice(number * BLOCK, (number + 1) * BLOCK)
            panel[first : first + BLOCK, first : first + inside] = stack[source, :inside]
            if inside < width:
                panel[first : first + BLOCK, : width - inside] = stack[source, inside:]

    for parity in range(2):

        @pl.when(core_ref[0] == parity)
        def _(parity=parity):
            copies = bring(partner_near, CHIPS[:NEAR], 1 - parity)
            place(own_near, CHIPS[:NEAR], parity)
            place(own_far, CHIPS[NEAR:], parity)
            place(partner_far, CHIPS[NEAR:], 1 - parity)
            for copy in copies:
                copy.wait()

    for block in range(blocks):
        own = slice(block * BLOCK, (block + 1) * BLOCK)
        for step in range(1, blocks - width // BLOCK + 1):
            other = (block + step) % blocks
            there = slice(other * BLOCK, (other + 1) * BLOCK)
            panel[there, own] = panel[own, there].T
    for at in range(0, col_count, TILE):
        product = jnp.dot(
            recoupled_ref[...], panel[:, at : at + TILE], preferred_element_type=jnp.float32
        )
        scaled[:, at : at + TILE] = (product * weight_ref[:, at : at + TILE]).astype(scaled.dtype)
    for at in range(0, col_count, TILE):
        picks = selection(order_ref[...], at)
        placed = lax.dot_general(
            scaled[...], picks, (((1,), (1,)), ((), ())), preferred_element_type=jnp.float32
        )
        restored[:, at : at + TILE] = placed.astype(restored.dtype)
    pack_body(restored, out_ref)


NEAR = 5
CHIPS = (0, -1, 1, -2, 2, -3, 3, 4)


def per_device(amplitudes, interaction, weights6j, column_order, row_counts):
    own_block = amplitudes[0]
    row_count, col_count = own_block.shape
    chan_count = lax.axis_size("chan")
    dtype = own_block.dtype
    packed_shape = (chan_count, row_count // 2, 128)
    packed = jax.ShapeDtypeStruct(packed_shape, dtype)
    flat = jax.ShapeDtypeStruct((row_count, col_count), dtype)
    blocks = col_count // BLOCK

    row_at = lax.axis_index("row")
    rows = lax.axis_size("row")
    core = row_at % 2
    half = jax.ShapeDtypeStruct((BLOCK, (blocks // 2 + 1) * BLOCK), dtype)
    own_half = call(halve_body, half, [smem(), vmem()])(row_at[None], interaction[0])

    def hop(far):
        return [(row, (row + 2 * far) % rows) for row in range(rows)]

    swap = [(row, row ^ 1) for row in range(rows)]
    sent = call(pack_body, packed, [vmem()])(own_block)
    from_below, from_above = [own_half], [own_half]
    for _ in range(3):
        from_below.append(lax.ppermute(from_below[-1], "row", hop(1)))
        from_above.append(lax.ppermute(from_above[-1], "row", hop(-1)))
    sent = near_core(sent)
    groups = lax.all_to_all(sent, "chan", split_axis=0, concat_axis=0, tiled=True)
    apart = list(zip(hop(1), hop(-1)))
    passed = jnp.where(core == 0, from_below[3], from_above[3])
    opposite = lax.ppermute(passed, "row", [pair[row % 2] for row, pair in enumerate(apart)])
    live_rows = row_counts - row_at * row_count
    recoupled, order, weight = call(
        recouple_body,
        (
            flat,
            jax.ShapeDtypeStruct(column_order.shape, column_order.dtype),
            jax.ShapeDtypeStruct(weights6j.shape, weights6j.dtype),
        ),
        [smem(), smem(), *[vmem()] * 3],
        [pltpu.VMEM(flat.shape, dtype)],
    )(live_rows, row_at[None], near_core(groups), column_order, weights6j)
    from_below[3], recoupled = lax.optimization_barrier((from_below[3], recoupled))
    pieces = [own_half]
    for pair in zip(from_below[1:], from_above[1:]):
        pieces += pair
    pieces.append(opposite)
    def stacked(some):
        shape = jax.ShapeDtypeStruct((len(some) * BLOCK, half.shape[1]), dtype)
        stack = near_core(call(stack_body, shape, [vmem()] * len(some))(*map(near_core, some)))
        return [stack, lax.ppermute(stack, "row", swap)]

    stacks = [*stacked(pieces[:NEAR]), *stacked(pieces[NEAR:])]
    stacks[3] = near_core(stacks[3])
    restored = call(
        product_body,
        packed,
        [smem(), *[vmem()] * 4, anywhere(), *[vmem()] * 2],
        [
            pltpu.VMEM((col_count, col_count), dtype),
            pltpu.VMEM(flat.shape, dtype),
            pltpu.VMEM(flat.shape, dtype),
            pltpu.SemaphoreType.DMA((2 * NEAR,)),
        ],
    )(core[None], near_core(recoupled), order, weight, *stacks)
    restored = near_core(restored)
    returned = lax.all_to_all(restored, "chan", split_axis=0, concat_axis=0, tiled=True)
    return call(unpack_body, flat, [vmem()])(near_core(returned))[None]


def solution(mesh):
    in_specs = (
        P("chan", "row", None),
        P("chan", "row", None),
        P("chan", None),
        P("chan", None),
        P("chan"),
    )
    out_specs = P("chan", "row", None)
    return jax.shard_map(
        per_device, mesh=mesh, in_specs=in_specs, out_specs=out_specs, check_vma=False
    )
```

```python
import jax
import jax.numpy as jnp
from jax import lax
from jax.experimental import pallas as pl
from jax.experimental.pallas import tpu as pltpu
from jax.sharding import PartitionSpec as P

VMEM_LIMIT = 28 * 1024 * 1024
TILE = 256
BLOCK = 128


def call(body, out_shape, in_specs, scratch=()):
    return pl.pallas_call(
        body,
        out_shape=out_shape,
        in_specs=in_specs,
        out_specs=jax.tree.map(lambda _: vmem(), out_shape),
        scratch_shapes=list(scratch),
        compiler_params=pltpu.CompilerParams(vmem_limit_bytes=VMEM_LIMIT),
    )


def near_core(array):
    return pltpu.with_memory_space_constraint(array, pltpu.VMEM)


def vmem():
    return pl.BlockSpec(memory_space=pltpu.VMEM)


def smem():
    return pl.BlockSpec(memory_space=pltpu.SMEM)


def anywhere():
    return pl.BlockSpec(memory_space=pl.ANY)


def swap_halves(upper, lower):
    low_lane = lax.broadcasted_iota(jnp.int32, upper.shape, 1) < 64
    first = jnp.where(low_lane, upper, pltpu.roll(lower, 64, 1))
    second = jnp.where(low_lane, pltpu.roll(upper, 64, 1), lower)
    return first, second


def pack_body(block_ref, out_ref):
    half = block_ref.shape[0] // 2
    for pair in range(out_ref.shape[0] // 2):
        lanes = pl.ds(pair * 128, 128)
        first, second = swap_halves(
            block_ref[:half, lanes].astype(jnp.float32), block_ref[half:, lanes].astype(jnp.float32)
        )
        out_ref[2 * pair] = first.astype(out_ref.dtype)
        out_ref[2 * pair + 1] = second.astype(out_ref.dtype)


def unpack_body(groups_ref, out_ref):
    half = groups_ref.shape[1]
    for pair in range(groups_ref.shape[0] // 2):
        lanes = pl.ds(pair * 128, 128)
        upper, lower = swap_halves(
            groups_ref[2 * pair].astype(jnp.float32), groups_ref[2 * pair + 1].astype(jnp.float32)
        )
        out_ref[:half, lanes] = upper.astype(out_ref.dtype)
        out_ref[half:, lanes] = lower.astype(out_ref.dtype)


def selection(order, first):
    rows = lax.broadcasted_iota(jnp.int32, (TILE, order.shape[1]), 0) + first
    return jnp.where(rows == order, 1.0, 0.0).astype(jnp.bfloat16)


def rotated(table_ref, first, out_ref):
    blocks = out_ref.shape[1] // BLOCK
    for step in range(blocks):
        at = pl.multiple_of((first + step) % blocks * BLOCK, BLOCK)
        out_ref[:, step * BLOCK : (step + 1) * BLOCK] = table_ref[:, pl.ds(at, BLOCK)]


def recouple_body(
    live_ref, row_ref, groups_ref, order_in, weight_in, out_ref, order_ref, weight_ref, gathered
):
    first = row_ref[0] - row_ref[0] % 2
    rotated(order_in, first, order_ref)
    rotated(weight_in, first, weight_ref)
    unpack_body(groups_ref, gathered)
    row_count, col_count = out_ref.shape
    live = lax.broadcasted_iota(jnp.int32, (row_count, TILE), 0) < live_ref[0]
    for at in range(0, col_count, TILE):
        order = order_ref[:, at : at + TILE]
        rows = lax.broadcasted_iota(jnp.int32, (col_count, TILE), 0)
        picks = jnp.where(rows == order, 1.0, 0.0).astype(jnp.bfloat16)
        taken = jnp.dot(gathered[...], picks, preferred_element_type=jnp.float32)
        taken = taken * weight_ref[:, at : at + TILE]
        out_ref[:, at : at + TILE] = jnp.where(live, taken, 0.0).astype(out_ref.dtype)


def halve_body(row_ref, panel_ref, out_ref):
    blocks = panel_ref.shape[1] // BLOCK
    for step in range(out_ref.shape[1] // BLOCK):
        at = pl.multiple_of((row_ref[0] + step) % blocks * BLOCK, BLOCK)
        out_ref[:, step * BLOCK : (step + 1) * BLOCK] = panel_ref[:, pl.ds(at, BLOCK)]


def stack_body(*refs):
    pieces, out_ref = refs[:-1], refs[-1]
    for number, piece in enumerate(pieces):
        out_ref[number * BLOCK : (number + 1) * BLOCK] = piece[...]


def product_body(core_ref, recoupled_ref, order_ref, weight_ref, *refs):
    row_count, col_count = recoupled_ref.shape
    blocks = col_count // BLOCK
    own_near, partner_near, own_far, partner_far, out_ref, panel, scaled, restored, sems = refs
    width = own_near.shape[1]

    def bring(stack, chips, parity):
        copies = []
        for number, chip in enumerate(chips):
            first = (2 * (chip % (blocks // 2)) + parity) * BLOCK
            inside = min(width, col_count - first)
            source, target = pl.ds(number * BLOCK, BLOCK), pl.ds(first, BLOCK)
            parts = [(0, first, inside)]
            if inside < width:
                parts.append((inside, 0, width - inside))
            for left, column, size in parts:
                copies.append(
                    pltpu.make_async_copy(
                        stack.at[source, pl.ds(left, size)],
                        panel.at[target, pl.ds(column, size)],
                        sems.at[len(copies)],
                    )
                )
        for copy in copies:
            copy.start()
        return copies

    def place(stack, chips, parity):
        for number, chip in enumerate(chips):
            first = (2 * (chip % (blocks // 2)) + parity) * BLOCK
            inside = min(width, col_count - first)
            source = slice(number * BLOCK, (number + 1) * BLOCK)
            panel[first : first + BLOCK, first : first + inside] = stack[source, :inside]
            if inside < width:
                panel[first : first + BLOCK, : width - inside] = stack[source, inside:]

    for parity in range(2):

        @pl.when(core_ref[0] == parity)
        def _(parity=parity):
            copies = bring(partner_near, CHIPS[:NEAR], 1 - parity)
            place(own_near, CHIPS[:NEAR], parity)
            place(own_far, CHIPS[NEAR:], parity)
            place(partner_far, CHIPS[NEAR:], 1 - parity)
            for copy in copies:
                copy.wait()

    for block in range(blocks):
        own = slice(block * BLOCK, (block + 1) * BLOCK)
        for step in range(1, blocks - width // BLOCK + 1):
            other = (block + step) % blocks
            there = slice(other * BLOCK, (other + 1) * BLOCK)
            panel[there, own] = panel[own, there].T
    for at in range(0, col_count, TILE):
        product = jnp.dot(
            recoupled_ref[...], panel[:, at : at + TILE], preferred_element_type=jnp.float32
        )
        scaled[:, at : at + TILE] = (product * weight_ref[:, at : at + TILE]).astype(scaled.dtype)
    for at in range(0, col_count, TILE):
        picks = selection(order_ref[...], at)
        placed = lax.dot_general(
            scaled[...], picks, (((1,), (1,)), ((), ())), preferred_element_type=jnp.float32
        )
        restored[:, at : at + TILE] = placed.astype(restored.dtype)
    pack_body(restored, out_ref)


NEAR = 4
CHIPS = (0, -1, 1, -2, 2, -3, 3, 4)


def per_device(amplitudes, interaction, weights6j, column_order, row_counts):
    own_block = amplitudes[0]
    row_count, col_count = own_block.shape
    chan_count = lax.axis_size("chan")
    dtype = own_block.dtype
    packed_shape = (chan_count, row_count // 2, 128)
    packed = jax.ShapeDtypeStruct(packed_shape, dtype)
    flat = jax.ShapeDtypeStruct((row_count, col_count), dtype)
    blocks = col_count // BLOCK

    row_at = lax.axis_index("row")
    rows = lax.axis_size("row")
    core = row_at % 2
    half = jax.ShapeDtypeStruct((BLOCK, (blocks // 2 + 1) * BLOCK), dtype)
    own_half = call(halve_body, half, [smem(), vmem()])(row_at[None], interaction[0])

    def hop(far):
        return [(row, (row + 2 * far) % rows) for row in range(rows)]

    swap = [(row, row ^ 1) for row in range(rows)]
    sent = call(pack_body, packed, [vmem()])(own_block)
    from_below, from_above = [own_half], [own_half]
    for _ in range(3):
        from_below.append(lax.ppermute(from_below[-1], "row", hop(1)))
        from_above.append(lax.ppermute(from_above[-1], "row", hop(-1)))
    sent = near_core(sent)
    groups = lax.all_to_all(sent, "chan", split_axis=0, concat_axis=0, tiled=True)
    apart = list(zip(hop(1), hop(-1)))
    passed = jnp.where(core == 0, from_below[3], from_above[3])
    opposite = lax.ppermute(passed, "row", [pair[row % 2] for row, pair in enumerate(apart)])
    live_rows = row_counts - row_at * row_count
    recoupled, order, weight = call(
        recouple_body,
        (
            flat,
            jax.ShapeDtypeStruct(column_order.shape, column_order.dtype),
            jax.ShapeDtypeStruct(weights6j.shape, weights6j.dtype),
        ),
        [smem(), smem(), *[vmem()] * 3],
        [pltpu.VMEM(flat.shape, dtype)],
    )(live_rows, row_at[None], near_core(groups), column_order, weights6j)
    from_below[3], recoupled = lax.optimization_barrier((from_below[3], recoupled))
    pieces = [own_half]
    for pair in zip(from_below[1:], from_above[1:]):
        pieces += pair
    pieces.append(opposite)
    def stacked(some):
        shape = jax.ShapeDtypeStruct((len(some) * BLOCK, half.shape[1]), dtype)
        stack = near_core(call(stack_body, shape, [vmem()] * len(some))(*map(near_core, some)))
        return [stack, lax.ppermute(stack, "row", swap)]

    stacks = [*stacked(pieces[:NEAR]), *stacked(pieces[NEAR:])]
    stacks[3] = near_core(stacks[3])
    restored = call(
        product_body,
        packed,
        [smem(), *[vmem()] * 4, anywhere(), *[vmem()] * 2],
        [
            pltpu.VMEM((col_count, col_count), dtype),
            pltpu.VMEM(flat.shape, dtype),
            pltpu.VMEM(flat.shape, dtype),
            pltpu.SemaphoreType.DMA((2 * NEAR,)),
        ],
    )(core[None], near_core(recoupled), order, weight, *stacks)
    restored = near_core(restored)
    returned = lax.all_to_all(restored, "chan", split_axis=0, concat_axis=0, tiled=True)
    return call(unpack_body, flat, [vmem()])(near_core(returned))[None]


def solution(mesh):
    in_specs = (
        P("chan", "row", None),
        P("chan", "row", None),
        P("chan", None),
        P("chan", None),
        P("chan"),
    )
    out_specs = P("chan", "row", None)
    return jax.shard_map(
        per_device, mesh=mesh, in_specs=in_specs, out_specs=out_specs, check_vma=False
    )
```
